32 devices in a mesh: rep: 4 (over x, core), dp: 8 (over z, y).
Axes of the slice: x: 2, y: 2, z: 4, core: 2. Of those that a mesh axis runs over, the one named last changes fastest.
Arguments:
- hidden: bfloat16 [2, 4, 4096, 1920], P(None, 'rep', 'dp'), may hold values from -6 to 6
- partners: int32 [2, 4], replicated, may hold values from 0 to 3, as said below
- frame_mask: int32 [2, 4096], P(None, 'dp'), may hold values 0 or 1
- segment_ids: int32 [2, 4096], P(None, 'dp'), may hold values from 0 to 7, as said below
- master: float32 [4, 1920, 500], P('rep', 'dp'), may hold values from -0.125 to 0.125
- moment_one: float32 [4, 1920, 500], P('rep', 'dp'), may hold values from -3 to 3
- moment_two: float32 [4, 1920, 500], P('rep', 'dp'), may hold values from 0.1 to 10
Outputs:
- hidden_grad: bfloat16 [2, 4, 4096, 1920], P(None, 'rep', 'dp')
- new_master: float32 [4, 1920, 500], P('rep', 'dp')
- new_moment_one: float32 [4, 1920, 500], P('rep', 'dp')
- new_moment_two: float32 [4, 1920, 500], P('rep', 'dp')
The draws below stay inside these ranges and needn't reach their ends.
Inputs may be any that keep to these rules, and one draw needn't show every extreme that they name: `partners`: each row is a permutation of the replicas forming one cycle through all of them, so no replica is its own partner. `segment_ids`: within each aligned block of 512 frames the ids start at 0 and never fall.
All inputs are finite; a program needn't handle non-finite values. No bound on the sum of `frame_mask` on one device may be relied on, other than what follows from the above.
Results may differ from the reference program's by a relative error of at most 0.035.
Values may be sent and summed in bfloat16 or wider, within the bound.
No kernel may reach another device: no remote copies, remote signals or barrier semaphores. Data moves between devices by JAX's collectives and lax.ppermute only.
A program may use at most 64 MiB of HBM per device.

```python
import math
import jax
import jax.numpy as jnp
from jax import lax

D = 1920
V = 500
SEGS = 8
TOK_DEV = 512
REPLICAS = 4
TOKENS = 4096


def draw_partners(key, part):
    result = []
    for micro in range(2):
        order = jax.random.permutation(jax.random.fold_in(key, 11 + micro), REPLICAS).astype(jnp.int32)
        following = jnp.roll(order, -1)
        result.append(jnp.zeros((REPLICAS,), jnp.int32).at[order].set(following))
    return jnp.stack(result)


def draw_segment_ids(key, part):
    blocks = TOKENS // TOK_DEV
    draws = jax.random.randint(jax.random.fold_in(key, 29), (2, blocks, TOK_DEV), 0, TOK_DEV)
    starts = (draws < SEGS - 1).astype(jnp.int32)
    starts = starts.at[:, :, 0].set(0)
    ids = jnp.minimum(jnp.cumsum(starts, axis=-1), SEGS - 1).astype(jnp.int32)
    return ids.reshape(2, TOKENS)


def set_ends(values, stream_key, least, high):
    place = [jax.random.randint(jax.random.fold_in(stream_key, axis), (), 0, length) for axis, length in enumerate(values.shape)]
    widest = values.shape.index(max(values.shape))
    beside = place[:widest] + [(place[widest] + 1) % values.shape[widest]] + place[widest + 1:]
    return values.at[tuple(place)].set(least).at[tuple(beside)].set(high)


def shard_levels(rng, dims, shards, least, largest):
    level, own = 1.0, jax.random.fold_in(rng, 6)
    for position, shards_of in shards:
        steps = jnp.exp(jax.random.uniform(jax.random.fold_in(own, position), (shards_of,), jnp.float32, least / len(shards), largest / len(shards)))
        level = level * jnp.repeat(steps, dims[position] // shards_of).reshape([-1 if axis == position else 1 for axis in range(len(dims))])
    return level


def bell_draw(own_key, dims, scale, bound, shards=(), held_as=jnp.bfloat16):
    loudness = shard_levels(own_key, dims, shards, -0.22, 0.18) if shards else 1.0
    values = jax.random.normal(own_key, dims, jnp.float32) * scale * loudness
    return jnp.minimum(jnp.maximum(values, -bound), bound).astype(held_as)


def setup_inputs(seed: int = 0) -> dict:
    key_list = jax.random.split(jax.random.key(seed), 8)
    return {
        "hidden": bell_draw(key_list[0], (2, REPLICAS, TOKENS, D), 1.0, 6.0, ((1, 4), (2, 8))),
        "partners": draw_partners(jax.random.fold_in(key_list[7], 71), 0),
        "frame_mask": set_ends((jax.random.randint(key_list[2], (2, TOKENS), 0, 4) < 3).astype(jnp.int32), jax.random.fold_in(key_list[2], 1), 0, 1),
        "segment_ids": draw_segment_ids(jax.random.fold_in(key_list[7], 71), 0),
        "master": bell_draw(key_list[4], (REPLICAS, D, V), D ** -0.5, 0.125, ((0, 4), (1, 8)), jnp.float32),
        "moment_one": bell_draw(key_list[5], (REPLICAS, D, V), 0.5, 3.0, ((0, 4), (1, 8)), jnp.float32),
        "moment_two": jnp.clip(jnp.exp(math.log(10.0) - 4.6051702 * jax.random.uniform(key_list[6], (REPLICAS, D, V), jnp.float32) ** shard_levels(key_list[6], (REPLICAS, D, V), ((0, 4), (1, 8)), -0.2, 0.2)), 0.1, 10.0),
    }


def frame_scale(frame_mask, segment_ids):
    blocks = TOKENS // TOK_DEV
    ids = segment_ids.reshape(2, blocks, TOK_DEV)
    valid = frame_mask.reshape(2, blocks, TOK_DEV).astype(jnp.float32)
    onehot = (ids[..., None] == jnp.arange(SEGS, dtype=jnp.int32)).astype(jnp.float32)
    counts = lax.optimization_barrier(jnp.sum(onehot * valid[..., None], axis=2))
    per_frame = lax.optimization_barrier(jnp.sum(onehot * counts[:, :, None, :], axis=-1))
    return (valid / jnp.maximum(per_frame, 1.0)).reshape(2, TOKENS)

def reference(hidden, partners, frame_mask, segment_ids, master, moment_one, moment_two):
    scale = frame_scale(frame_mask, segment_ids)
    head_low = master.astype(jnp.bfloat16)
    logits = jnp.stack([jnp.stack([jnp.dot(hidden[m, r], head_low[r], preferred_element_type=jnp.float32) for r in range(REPLICAS)]) for m in range(2)])
    sent = logits.astype(jnp.bfloat16)
    grads_out = []
    hidden_out = []
    for m in range(2):
        other = jnp.take(sent[m], partners[m].astype(jnp.int32), axis=0).astype(jnp.float32)
        grad = ((logits[m] - other) * scale[m][None, :, None]).astype(jnp.bfloat16)
        grads_out.append(grad)
        hidden_out.append(jnp.stack([jnp.dot(grad[r], head_low[r].T, preferred_element_type=jnp.float32).astype(jnp.bfloat16) for r in range(REPLICAS)]))
    hidden_grad = jnp.stack(hidden_out)
    head_grad = jnp.stack([jnp.dot(hidden[0, r].T, grads_out[0][r], preferred_element_type=jnp.float32) + jnp.dot(hidden[1, r].T, grads_out[1][r], preferred_element_type=jnp.float32) for r in range(REPLICAS)])
    new_moment_one = 0.9 * moment_one + 0.1 * head_grad
    new_moment_two = 0.99 * moment_two + 0.01 * head_grad * head_grad
    new_master = master - 0.01 * new_moment_one / (jnp.sqrt(new_moment_two) + 1e-08)
    return (hidden_grad, new_master, new_moment_one, new_moment_two)
```

```python
import jax
import jax.numpy as jnp
from jax import lax
from jax.sharding import PartitionSpec as P

SEGS = 8


def ring_of(n):
    return list(range(0, n, 2)) + list(range(n - 1 - (n % 2), 0, -2))


class Ring:
    def __init__(self, axis, n):
        order = ring_of(n)
        self.axis, self.n = axis, n
        self.up = [(order[i], order[(i + 1) % n]) for i in range(n)]
        self.down = [(b, a) for a, b in self.up]
        place = [0] * n
        for i, d in enumerate(order):
            place[d] = i
        self.order = jnp.array(order, jnp.int32)
        self.pos = jnp.array(place, jnp.int32)[lax.axis_index(axis)]

    def owner(self, offset):
        return self.order[(self.pos + offset + self.n) % self.n]

    def gather(self, block):
        n, rows = self.n, block.shape[0]
        found = [(0, 0, block)]
        ahead = behind = block
        for step in range(1, (n - 1) // 2 + 1):
            ahead = lax.ppermute(ahead, self.axis, self.up)
            behind = lax.ppermute(behind, self.axis, self.down)
            found += [(-step, 0, ahead), (step, 0, behind)]
        if n % 2 == 0:
            half = rows // 2
            far = n // 2
            found.append((-far, 0, lax.ppermute(ahead[:half], self.axis, self.up)))
            found.append((far, half, lax.ppermute(behind[half:], self.axis, self.down)))
        return found

    def assemble(self, found, rows):
        whole = jnp.zeros((self.n * rows, found[0][2].shape[1]), found[0][2].dtype)
        for offset, start, block in found:
            whole = lax.dynamic_update_slice(whole, block, (self.owner(offset) * rows + start, 0))
        return whole

    def scatter_sum(self, terms, rows):
        n = self.n

        def mine(offset, start=0, size=rows):
            return lax.dynamic_slice(terms, (self.owner(offset) * rows + start, 0), (size, terms.shape[1]))

        ahead = behind = None
        steps = (n - 1) // 2
        if n % 2 == 0:
            half, far = rows // 2, n // 2
            ahead = lax.ppermute(mine(far, 0, half), self.axis, self.up)
            behind = lax.ppermute(mine(-far, half, rows - half), self.axis, self.down)
            ahead = jnp.concatenate([ahead, jnp.zeros((rows - half, terms.shape[1]), terms.dtype)])
            behind = jnp.concatenate([jnp.zeros((half, terms.shape[1]), terms.dtype), behind])
        for step in range(steps, 0, -1):
            up, down = mine(step), mine(-step)
            if ahead is not None:
                up, down = up + ahead, down + behind
            ahead = lax.ppermute(up, self.axis, self.up)
            behind = lax.ppermute(down, self.axis, self.down)
        return mine(0).astype(jnp.float32) + ahead.astype(jnp.float32) + behind.astype(jnp.float32)


def partner_values(sent, partners, replicas):
    chips = replicas // 2
    mine = lax.axis_index("rep")
    chip, core = mine // 2, mine % 2
    near = [sent]
    for s in range(1, chips):
        near.append(lax.ppermute(sent, "rep", [(r, (r + 2 * s) % replicas) for r in range(replicas)]))

    def pick(wanted):
        back = (chip - wanted // 2 + chips) % chips
        out = near[0]
        for s in range(1, chips):
            out = jnp.where((back == s)[:, None, None], near[s], out)
        return out

    across = lax.ppermute(pick(partners[:, mine ^ 1]), "rep", [(r, r ^ 1) for r in range(replicas)])
    wanted = partners[:, mine]
    return jnp.where((wanted % 2 == core)[:, None, None], pick(wanted), across)


def step(replicas, shards, hidden, partners, frame_mask, segment_ids, master, moment_one, moment_two):
    frames, features = hidden.shape[2], hidden.shape[3]
    rows, classes = master.shape[1], master.shape[2]
    ring = Ring("dp", shards)
    frames_all = hidden[:, 0].reshape(2 * frames, features)
    head_low = master[0].astype(jnp.bfloat16)
    cut = 256 if classes > 256 else classes
    spans = [(a, min(a + cut, classes)) for a in range(0, classes, cut)]

    valid = frame_mask.astype(jnp.float32)
    onehot = (segment_ids[..., None] == jnp.arange(SEGS, dtype=jnp.int32)).astype(jnp.float32)
    counts = jnp.sum(onehot * valid[..., None], axis=1)
    per_frame = jnp.sum(onehot * counts[:, None, :], axis=-1)
    scale = valid / jnp.maximum(per_frame, 1.0)

    heads, grads, sums = [], [], []
    for a, b in spans:
        heads.append(ring.assemble(ring.gather(head_low[:, a:b]), rows))
    for (a, b), head in zip(spans, heads):
        logits = jnp.dot(frames_all, head, preferred_element_type=jnp.float32).reshape(2, frames, b - a)
        other = partner_values(logits.astype(jnp.bfloat16), partners, replicas)
        grad = ((logits - other.astype(jnp.float32)) * scale[:, :, None]).astype(jnp.bfloat16)
        grad = grad.reshape(2 * frames, b - a)
        grads.append(grad)
        terms = jnp.einsum("td,tv->dv", frames_all, grad, preferred_element_type=jnp.float32).astype(jnp.bfloat16)
        sums.append(ring.scatter_sum(terms, rows))
    hidden_grad = jnp.einsum(
        "tv,dv->td",
        jnp.concatenate(grads, axis=1),
        jnp.concatenate(heads, axis=1),
        preferred_element_type=jnp.float32,
    )
    hidden_grad = hidden_grad.astype(jnp.bfloat16).reshape(2, 1, frames, features)
    head_grad = jnp.concatenate(sums, axis=1)[None]
    new_moment_one = 0.9 * moment_one + 0.1 * head_grad
    new_moment_two = 0.99 * moment_two + 0.01 * head_grad * head_grad
    new_master = master - 0.01 * new_moment_one / (jnp.sqrt(new_moment_two) + 1e-08)
    return hidden_grad, new_master, new_moment_one, new_moment_two


def solution(mesh):
    replicas, shards = mesh.shape["rep"], mesh.shape["dp"]
    whole = P("rep", "dp", None)
    return jax.shard_map(
        lambda *args: step(replicas, shards, *args),
        mesh=mesh,
        in_specs=(P(None, "rep", "dp", None), P(), P(None, "dp"), P(None, "dp"), whole, whole, whole),
        out_specs=(P(None, "rep", "dp", None), whole, whole, whole),
        check_vma=False,
    )
```

```python
import jax
import jax.numpy as jnp
from jax import lax
from jax.experimental import pallas as pl
from jax.experimental.pallas import tpu as pltpu
from jax.sharding import PartitionSpec as P


SEGS = 8
LANES = 128
F32, BF16 = jnp.float32, jnp.bfloat16
VMEM = pl.BlockSpec(memory_space=pltpu.VMEM)
SMEM = pl.BlockSpec(memory_space=pltpu.SMEM)
SMALL = pltpu.CompilerParams(vmem_limit_bytes=12 << 20)


def cost(flops, nbytes):
    return pl.CostEstimate(flops=flops, bytes_accessed=nbytes, transcendentals=0)


def shape(dims, dtype):
    return jax.ShapeDtypeStruct(dims, dtype)


class Ring:
    def __init__(self, axis, n):
        order = list(range(0, n, 2)) + list(range(n - 1 - (n % 2), 0, -2))
        self.axis, self.n = axis, n
        self.up = [(order[i], order[(i + 1) % n]) for i in range(n)]
        self.down = [(b, a) for a, b in self.up]

    def owner(self, k):
        n, d = self.n, lax.axis_index(self.axis)
        place = jnp.where(d % 2 == 0, d // 2, n - 1 - d // 2)
        at = (place + k) % n
        return jnp.where(at < (n + 1) // 2, 2 * at, 2 * (n - at) - 1)

    def steps(self, up_longer):
        n = self.n
        return (n // 2, (n - 1) // 2) if up_longer else ((n - 1) // 2, n // 2)

    def send_up(self, x):
        return lax.ppermute(x, self.axis, self.up)

    def send_down(self, x):
        return lax.ppermute(x, self.axis, self.down)

    def gather(self, block, up_longer):
        ups, downs = self.steps(up_longer)
        found = {0: block}
        ahead = behind = block
        for step in range(1, max(ups, downs) + 1):
            if step <= ups:
                ahead = self.send_up(ahead)
                found[self.n - step] = ahead
            if step <= downs:
                behind = self.send_down(behind)
                found[step] = behind
        return [found[k] for k in range(self.n)]

    def scatter_sum(self, terms, up_longer):
        ups, downs = self.steps(up_longer)
        ahead = behind = None
        for step in range(max(ups, downs), 0, -1):
            if step <= ups:
                out = terms[step] if ahead is None else terms[step] + ahead
                ahead = self.send_up(out)
            if step <= downs:
                out = terms[self.n - step] if behind is None else terms[self.n - step] + behind
                behind = self.send_down(out)
        return [terms[0], ahead, behind]


def round_head(master, spans):
    def body(src, *outs):
        for (a, b), out in zip(spans, outs):
            out[...] = src[0, :, a:b].astype(BF16)

    rows = master.shape[1]
    return pl.pallas_call(
        body,
        out_shape=[shape((rows, b - a), BF16) for a, b in spans],
        in_specs=[VMEM],
        out_specs=[VMEM] * len(spans),
        cost_estimate=cost(0, master.size * 6),
        compiler_params=SMALL,
        name="round_head",
    )(master)


def frame_scales(frame_mask, segment_ids):
    micro, frames = frame_mask.shape

    def body(mask, ids, out):
        for m in range(micro):
            valid = mask[m : m + 1, :].astype(F32)
            own = ids[m : m + 1, :]
            per_frame = jnp.zeros_like(valid)
            for s in range(SEGS):
                hit = (own == s).astype(F32)
                per_frame += hit * jnp.sum(hit * valid, axis=1, keepdims=True)
            scale = valid / jnp.maximum(per_frame, 1.0)
            out[m * frames : (m + 1) * frames, :] = jnp.broadcast_to(scale, (LANES, frames)).T

    return pl.pallas_call(
        body,
        out_shape=shape((micro * frames, LANES), F32),
        in_specs=[VMEM, VMEM],
        out_specs=VMEM,
        cost_estimate=cost(0, micro * frames * LANES * 4),
        compiler_params=SMALL,
        name="frame_scales",
    )(frame_mask, segment_ids)


def transposed(x):
    rows, columns = x.shape
    tile = next(t for t in (640, 512, 384, 256, 128) if columns % t == 0)

    def body(src, out):
        for at in range(0, columns, tile):
            out[at : at + tile, :] = src[:, at : at + tile].T

    return pl.pallas_call(
        body,
        out_shape=shape((columns, rows), x.dtype),
        in_specs=[VMEM],
        out_specs=VMEM,
        compiler_params=SMALL,
        cost_estimate=cost(0, x.size * 4),
        name="transposed",
    )(x)


def logits_of(frames_all, blocks, owner, tile=512):
    tokens, features = frames_all.shape
    rows, classes = blocks[0].shape
    tile = min(tile, tokens)

    def body(x, *refs):
        parts, (kept, logits, sent, head, sem) = refs[: len(blocks)], refs[len(blocks) :]
        for k, part in enumerate(parts):
            at = pl.multiple_of(owner(k) * rows, 16)
            head[pl.ds(at, rows), :] = part[...]
        keep = pltpu.make_async_copy(head, kept, sem)
        keep.start()
        for at in range(0, tokens, tile):
            value = jnp.dot(x[at : at + tile, :], head[...], preferred_element_type=F32)
            logits[at : at + tile, :] = value
            sent[at : at + tile, :] = value.astype(BF16)
        keep.wait()

    return pl.pallas_call(
        body,
        out_shape=[shape((features, classes), BF16), shape((tokens, classes), F32), shape((tokens, classes), BF16)],
        in_specs=[VMEM] * (1 + len(blocks)),
        out_specs=[pl.BlockSpec(memory_space=pltpu.HBM), VMEM, VMEM],
        scratch_shapes=[pltpu.VMEM((features, classes), BF16), pltpu.SemaphoreType.DMA],
        compiler_params=SMALL,
        cost_estimate=cost(2 * tokens * features * classes, tokens * features * 2),
        name="logits_of",
    )(frames_all, *blocks)


def gradient(partners, logits, candidates, scales, replicas):
    tokens, classes = logits.shape
    micro, chips = partners.shape[0], replicas // 2
    frames = tokens // micro

    def body(partners_ref, logits_ref, scale_ref, *refs):
        options, out = refs[:-1], refs[-1]
        mine = lax.axis_index("rep")
        for m in range(micro):
            here = slice(m * frames, (m + 1) * frames)
            wanted = partners_ref[m, mine]
            back = (mine // 2 - wanted // 2 + chips) % chips
            choice = jnp.where(wanted % 2 == mine % 2, back - 1, back + chips - 1)
            for k, option in enumerate(options):

                @pl.when(choice == k)
                def _(option=option, here=here):
                    for a in range(0, classes, LANES):
                        b = min(a + LANES, classes)
                        gap = logits_ref[here, a:b] - option[here, a:b].astype(F32)
                        out[here, a:b] = (gap * scale_ref[here, : b - a]).astype(BF16)

    return pl.pallas_call(
        body,
        out_shape=shape((tokens, classes), BF16),
        in_specs=[SMEM] + [VMEM] * (2 + len(candidates)),
        out_specs=VMEM,
        compiler_params=SMALL,
        cost_estimate=cost(3 * tokens * classes, tokens * classes * 8),
        name="gradient",
    )(partners, logits, scales, *candidates)


def head_terms(turned, grad, owner, places, rows):
    tokens, classes = grad.shape

    def body(turned_ref, grad_ref, *outs):
        for k, out in zip(places, outs):
            at = pl.multiple_of(owner(k) * rows, 16)
            term = jnp.dot(turned_ref[pl.ds(at, rows), :], grad_ref[...], preferred_element_type=F32)
            out[...] = term.astype(BF16)

    return pl.pallas_call(
        body,
        out_shape=[shape((rows, classes), BF16)] * len(places),
        in_specs=[VMEM, VMEM],
        out_specs=[VMEM] * len(places),
        compiler_params=SMALL,
        cost_estimate=cost(2 * tokens * rows * classes * len(places), len(places) * rows * tokens * 2),
        name="head_terms",
    )(turned, grad)


def hidden_gradient(grads, heads, tile=256):
    tokens, features = grads[0].shape[0], heads[0].shape[0]
    count = len(grads)

    def body(*refs):
        out = refs[-1]
        total = None
        for g, h in zip(refs[:count], refs[count:-1]):
            term = lax.dot_general(g[...], h[...], (((1,), (1,)), ((), ())), preferred_element_type=F32)
            total = term if total is None else total + term
        out[...] = total.astype(BF16)

    classes = sum(g.shape[1] for g in grads)
    return pl.pallas_call(
        body,
        out_shape=shape((tokens, features), BF16),
        grid=(tokens // tile,),
        in_specs=[pl.BlockSpec((tile, g.shape[1]), lambda i: (i, 0)) for g in grads]
        + [pl.BlockSpec(h.shape, lambda i: (0, 0)) for h in heads],
        out_specs=pl.BlockSpec((tile, features), lambda i: (i, 0)),
        cost_estimate=cost(2 * tokens * features * classes, tokens * features * 2),
        compiler_params=SMALL,
        name="hidden_gradient",
    )(*grads, *heads)


def adam(sums, spans, master, moment_one, moment_two):
    each = len(sums[0])
    flat = [x for group in sums for x in group]

    def body(*refs):
        terms, (w, one, two, new_w, new_one, new_two) = refs[: len(flat)], refs[len(flat) :]
        for i, (a, b) in enumerate(spans):
            g = sum(t[...].astype(F32) for t in terms[i * each : (i + 1) * each])
            first = 0.9 * one[0, :, a:b] + 0.1 * g
            second = 0.99 * two[0, :, a:b] + 0.01 * g * g
            new_one[0, :, a:b] = first
            new_two[0, :, a:b] = second
            new_w[0, :, a:b] = w[0, :, a:b] - 0.01 * first / (jnp.sqrt(second) + 1e-08)

    out = shape(master.shape, F32)
    return pl.pallas_call(
        body,
        out_shape=[out, out, out],
        in_specs=[VMEM] * (len(flat) + 3),
        out_specs=[VMEM] * 3,
        cost_estimate=cost(12 * master.size, 24 * master.size),
        compiler_params=SMALL,
        name="adam",
    )(*flat, master, moment_one, moment_two)


def across_replicas(sent, replicas):
    chips = replicas // 2
    swap = [(r, r ^ 1) for r in range(replicas)]
    far, near = [], []
    for s in range(1, chips):
        far.append(lax.ppermute(sent, "rep", [(r, (r + 2 * s) % replicas) for r in range(replicas)]))
    for x in [sent] + far:
        near.append(lax.ppermute(x, "rep", swap))
    return far + near


def step(replicas, shards, hidden, partners, frame_mask, segment_ids, master, moment_one, moment_two):
    micro, _, frames, features = hidden.shape
    rows, classes = master.shape[1], master.shape[2]
    aligned = rows % 16 == 0
    ring = Ring("dp", shards)
    frames_all = hidden.reshape(micro * frames, features)
    cut = 2 * LANES
    spans = [(a, min(a + cut, classes)) for a in range(0, classes, cut)]

    scales = frame_scales(frame_mask, segment_ids)
    turned = transposed(frames_all)
    low = round_head(master, spans)
    heads, grads, sums = [], [], []
    gathered = [ring.gather(x, i % 2 == 0) for i, x in enumerate(low)]
    for i, blocks in enumerate(gathered):
        longer = i % 2 == 0
        if aligned:
            head, logits, sent = logits_of(frames_all, blocks, ring.owner)
        else:
            whole = jnp.zeros((features, blocks[0].shape[1]), BF16)
            for k, block in enumerate(blocks):
                whole = lax.dynamic_update_slice(whole, block, (ring.owner(k) * rows, 0))
            head, logits, sent = logits_of(frames_all, [whole], lambda k: 0)
        others = across_replicas(sent, replicas)
        grad = gradient(partners, logits, others, scales, replicas)
        ups, downs = ring.steps(longer)
        first = sorted({ups, shards - downs})
        rest = [k for k in range(shards) if k not in first]
        if aligned:
            found = dict(zip(first, head_terms(turned, grad, ring.owner, first, rows)))
            found.update(zip(rest, head_terms(turned, grad, ring.owner, rest, rows)))
        else:
            product = jnp.dot(turned, grad, preferred_element_type=F32).astype(BF16)
            found = {
                k: lax.dynamic_slice(product, (ring.owner(k) * rows, 0), (rows, grad.shape[1])) for k in range(shards)
            }
        heads.append(head)
        grads.append(grad)
        sums.append(ring.scatter_sum([found[k] for k in range(shards)], longer))
    hidden_grad = hidden_gradient(grads, heads).reshape(hidden.shape)
    return (hidden_grad, *adam(sums, spans, master, moment_one, moment_two))


def solution(mesh):
    whole = P("rep", "dp", None)
    replicas, shards = mesh.shape["rep"], mesh.shape["dp"]

    def program(*args):
        return step(replicas, shards, *args)

    return jax.shard_map(
        program,
        mesh=mesh,
        in_specs=(P(None, "rep", "dp", None), P(), P(None, "dp"), P(None, "dp"), whole, whole, whole),
        out_specs=(P(None, "rep", "dp", None), whole, whole, whole),
        check_vma=False,
    )
```

```python
import jax
import jax.numpy as jnp
from jax import lax
from jax.experimental import pallas as pl
from jax.experimental.pallas import tpu as pltpu
from jax.sharding import PartitionSpec as P


SEGS = 8
LANES = 128
F32, BF16 = jnp.float32, jnp.bfloat16
VMEM = pl.BlockSpec(memory_space=pltpu.VMEM)
SMEM = pl.BlockSpec(memory_space=pltpu.SMEM)
SMALL = pltpu.CompilerParams(vmem_limit_bytes=12 << 20)


def cost(flops, nbytes):
    return pl.CostEstimate(flops=flops, bytes_accessed=nbytes, transcendentals=0)


def shape(dims, dtype):
    return jax.ShapeDtypeStruct(dims, dtype)


class Ring:
    def __init__(self, axis, n):
        order = list(range(0, n, 2)) + list(range(n - 1 - (n % 2), 0, -2))
        self.axis, self.n = axis, n
        self.up = [(order[i], order[(i + 1) % n]) for i in range(n)]
        self.down = [(b, a) for a, b in self.up]

    def owner(self, k):
        n, d = self.n, lax.axis_index(self.axis)
        place = jnp.where(d % 2 == 0, d // 2, n - 1 - d // 2)
        at = (place + k) % n
        return jnp.where(at < (n + 1) // 2, 2 * at, 2 * (n - at) - 1)

    def steps(self, up_longer):
        n = self.n
        return (n // 2, (n - 1) // 2) if up_longer else ((n - 1) // 2, n // 2)

    def send_up(self, x):
        return lax.ppermute(x, self.axis, self.up)

    def send_down(self, x):
        return lax.ppermute(x, self.axis, self.down)

    def gather(self, block, up_longer):
        ups, downs = self.steps(up_longer)
        found = {0: block}
        ahead = behind = block
        for step in range(1, max(ups, downs) + 1):
            if step <= ups:
                ahead = self.send_up(ahead)
                found[self.n - step] = ahead
            if step <= downs:
                behind = self.send_down(behind)
                found[step] = behind
        return [found[k] for k in range(self.n)]

    def scatter_sum(self, terms, up_longer):
        ups, downs = self.steps(up_longer)
        ahead = behind = None
        for step in range(max(ups, downs), 0, -1):
            if step <= ups:
                out = terms[step] if ahead is None else terms[step] + ahead
                ahead = self.send_up(out)
            if step <= downs:
                out = terms[self.n - step] if behind is None else terms[self.n - step] + behind
                behind = self.send_down(out)
        return [terms[0], ahead, behind]


def round_head(master, spans):
    def body(src, *outs):
        for (a, b), out in zip(spans, outs):
            out[...] = src[0, :, a:b].astype(BF16)

    rows = master.shape[1]
    return pl.pallas_call(
        body,
        out_shape=[shape((rows, b - a), BF16) for a, b in spans],
        in_specs=[VMEM],
        out_specs=[VMEM] * len(spans),
        cost_estimate=cost(0, master.size * 6),
        compiler_params=SMALL,
        name="round_head",
    )(master)


def frame_scales(frame_mask, segment_ids):
    micro, frames = frame_mask.shape

    def body(mask, ids, out):
        for m in range(micro):
            valid = mask[m : m + 1, :].astype(F32)
            own = ids[m : m + 1, :]
            per_frame = jnp.zeros_like(valid)
            for s in range(SEGS):
                hit = (own == s).astype(F32)
                per_frame += hit * jnp.sum(hit * valid, axis=1, keepdims=True)
            scale = valid / jnp.maximum(per_frame, 1.0)
            out[m * frames : (m + 1) * frames, :] = jnp.broadcast_to(scale, (LANES, frames)).T

    return pl.pallas_call(
        body,
        out_shape=shape((micro * frames, LANES), F32),
        in_specs=[VMEM, VMEM],
        out_specs=VMEM,
        cost_estimate=cost(0, micro * frames * LANES * 4),
        compiler_params=SMALL,
        name="frame_scales",
    )(frame_mask, segment_ids)


def transposed(x):
    rows, columns = x.shape
    tile = next(t for t in (640, 512, 384, 256, 128) if columns % t == 0)

    def body(src, out):
        for at in range(0, columns, tile):
            out[at : at + tile, :] = src[:, at : at + tile].T

    return pl.pallas_call(
        body,
        out_shape=shape((columns, rows), x.dtype),
        in_specs=[VMEM],
        out_specs=VMEM,
        compiler_params=SMALL,
        cost_estimate=cost(0, x.size * 4),
        name="transposed",
    )(x)


def logits_of(frames_all, blocks, owner, tile=512):
    tokens, features = frames_all.shape
    rows, classes = blocks[0].shape
    tile = min(tile, tokens)

    def body(x, *refs):
        parts, (kept, logits, sent, head, sem) = refs[: len(blocks)], refs[len(blocks) :]
        for k, part in enumerate(parts):
            at = pl.multiple_of(owner(k) * rows, 16)
            head[pl.ds(at, rows), :] = part[...]
        keep = pltpu.make_async_copy(head, kept, sem)
        keep.start()
        for at in range(0, tokens, tile):
            value = jnp.dot(x[at : at + tile, :], head[...], preferred_element_type=F32)
            logits[at : at + tile, :] = value
            sent[at : at + tile, :] = value.astype(BF16)
        keep.wait()

    return pl.pallas_call(
        body,
        out_shape=[shape((features, classes), BF16), shape((tokens, classes), F32), shape((tokens, classes), BF16)],
        in_specs=[VMEM] * (1 + len(blocks)),
        out_specs=[pl.BlockSpec(memory_space=pltpu.HBM), VMEM, VMEM],
        scratch_shapes=[pltpu.VMEM((features, classes), BF16), pltpu.SemaphoreType.DMA],
        compiler_params=SMALL,
        cost_estimate=cost(2 * tokens * features * classes, tokens * features * 2),
        name="logits_of",
    )(frames_all, *blocks)


def gradient(partners, logits, candidates, scales, replicas):
    tokens, classes = logits.shape
    micro, chips = partners.shape[0], replicas // 2
    frames = tokens // micro

    def body(partners_ref, logits_ref, scale_ref, *refs):
        options, out = refs[:-1], refs[-1]
        mine = lax.axis_index("rep")
        for m in range(micro):
            here = slice(m * frames, (m + 1) * frames)
            wanted = partners_ref[m, mine]
            back = (mine // 2 - wanted // 2 + chips) % chips
            choice = jnp.where(wanted % 2 == mine % 2, back - 1, back + chips - 1)
            for k, option in enumerate(options):

                @pl.when(choice == k)
                def _(option=option, here=here):
                    for a in range(0, classes, LANES):
                        b = min(a + LANES, classes)
                        gap = logits_ref[here, a:b] - option[here, a:b].astype(F32)
                        out[here, a:b] = (gap * scale_ref[here, : b - a]).astype(BF16)

    return pl.pallas_call(
        body,
        out_shape=shape((tokens, classes), BF16),
        in_specs=[SMEM] + [VMEM] * (2 + len(candidates)),
        out_specs=VMEM,
        compiler_params=SMALL,
        cost_estimate=cost(3 * tokens * classes, tokens * classes * 8),
        name="gradient",
    )(partners, logits, scales, *candidates)


def head_terms(turned, grad, owner, places, rows):
    tokens, classes = grad.shape

    def body(turned_ref, grad_ref, *outs):
        for k, out in zip(places, outs):
            at = pl.multiple_of(owner(k) * rows, 16)
            term = jnp.dot(turned_ref[pl.ds(at, rows), :], grad_ref[...], preferred_element_type=F32)
            out[...] = term.astype(BF16)

    return pl.pallas_call(
        body,
        out_shape=[shape((rows, classes), BF16)] * len(places),
        in_specs=[VMEM, VMEM],
        out_specs=[VMEM] * len(places),
        compiler_params=SMALL,
        cost_estimate=cost(2 * tokens * rows * classes * len(places), len(places) * rows * tokens * 2),
        name="head_terms",
    )(turned, grad)


def hidden_gradient(grads, heads, tile=512):
    tokens, features = grads[0].shape[0], heads[0].shape[0]
    count = len(grads)

    def body(*refs):
        out = refs[-1]
        total = None
        for g, h in zip(refs[:count], refs[count:-1]):
            term = lax.dot_general(g[...], h[...], (((1,), (1,)), ((), ())), preferred_element_type=F32)
            total = term if total is None else total + term
        out[...] = total.astype(BF16)

    classes = sum(g.shape[1] for g in grads)
    return pl.pallas_call(
        body,
        out_shape=shape((tokens, features), BF16),
        grid=(tokens // tile,),
        in_specs=[pl.BlockSpec((tile, g.shape[1]), lambda i: (i, 0)) for g in grads]
        + [pl.BlockSpec(h.shape, lambda i: (0, 0)) for h in heads],
        out_specs=pl.BlockSpec((tile, features), lambda i: (i, 0)),
        cost_estimate=cost(2 * tokens * features * classes, tokens * features * 2),
        compiler_params=SMALL,
        name="hidden_gradient",
    )(*grads, *heads)


def adam(terms, span, master, moment_one, moment_two, before):
    a, b = span
    rows = master.shape[1]
    count = len(terms)

    def body(*refs):
        parts, (w, one, two) = refs[:count], refs[count : count + 3]
        outs, staged, sems = refs[-7:-4], refs[-4:-1], refs[-1]
        g = sum(t[...].astype(F32) for t in parts)
        first = 0.9 * one[0, :, a:b] + 0.1 * g
        second = 0.99 * two[0, :, a:b] + 0.01 * g * g
        copies = [
            pltpu.make_async_copy(held, out.at[0, :, a:b], sems.at[i]) for i, (held, out) in enumerate(zip(staged, outs))
        ]
        staged[1][...] = first
        copies[1].start()
        staged[2][...] = second
        copies[2].start()
        staged[0][...] = w[0, :, a:b] - 0.01 * first / (jnp.sqrt(second) + 1e-08)
        copies[0].start()
        for copy in copies:
            copy.wait()

    hbm = pl.BlockSpec(memory_space=pltpu.HBM)
    return pl.pallas_call(
        body,
        out_shape=[shape(master.shape, F32)] * 3,
        in_specs=[VMEM] * (count + 3) + [hbm] * len(before),
        out_specs=[hbm] * 3,
        scratch_shapes=[pltpu.VMEM((rows, b - a), F32)] * 3 + [pltpu.SemaphoreType.DMA((3,))],
        input_output_aliases={count + 3 + i: i for i in range(len(before))},
        cost_estimate=cost(12 * rows * (b - a), 24 * rows * (b - a)),
        compiler_params=SMALL,
        name="adam",
    )(*terms, master, moment_one, moment_two, *before)


def across_replicas(sent, replicas):
    chips = replicas // 2
    swap = [(r, r ^ 1) for r in range(replicas)]
    far, near = [], []
    for s in range(1, chips):
        far.append(lax.ppermute(sent, "rep", [(r, (r + 2 * s) % replicas) for r in range(replicas)]))
    for x in [sent] + far:
        near.append(lax.ppermute(x, "rep", swap))
    return far + near


def step(replicas, shards, hidden, partners, frame_mask, segment_ids, master, moment_one, moment_two):
    micro, _, frames, features = hidden.shape
    rows, classes = master.shape[1], master.shape[2]
    aligned = rows % 16 == 0
    ring = Ring("dp", shards)
    frames_all = hidden.reshape(micro * frames, features)
    cut = 2 * LANES
    spans = [(a, min(a + cut, classes)) for a in range(0, classes, cut)]

    scales = frame_scales(frame_mask, segment_ids)
    turned = transposed(frames_all)
    low = round_head(master, spans)
    heads, grads, sums = [], [], []
    gathered = [ring.gather(x, i % 2 == 0) for i, x in enumerate(low)]
    for i, blocks in enumerate(gathered):
        longer = i % 2 == 0
        if aligned:
            head, logits, sent = logits_of(frames_all, blocks, ring.owner)
        else:
            whole = jnp.zeros((features, blocks[0].shape[1]), BF16)
            for k, block in enumerate(blocks):
                whole = lax.dynamic_update_slice(whole, block, (ring.owner(k) * rows, 0))
            head, logits, sent = logits_of(frames_all, [whole], lambda k: 0)
        others = across_replicas(sent, replicas)
        grad = gradient(partners, logits, others, scales, replicas)
        ups, downs = ring.steps(longer)
        first = sorted({ups, shards - downs})
        rest = [k for k in range(shards) if k not in first]
        if aligned:
            found = dict(zip(first, head_terms(turned, grad, ring.owner, first, rows)))
            found.update(zip(rest, head_terms(turned, grad, ring.owner, rest, rows)))
        else:
            product = jnp.dot(turned, grad, preferred_element_type=F32).astype(BF16)
            found = {
                k: lax.dynamic_slice(product, (ring.owner(k) * rows, 0), (rows, grad.shape[1])) for k in range(shards)
            }
        heads.append(head)
        grads.append(grad)
        sums.append(ring.scatter_sum([found[k] for k in range(shards)], longer))
    hidden_grad = hidden_gradient(grads, heads).reshape(hidden.shape)
    new = ()
    for i, span in enumerate(spans):
        new = adam(sums[i], span, master, moment_one, moment_two, new)
    return (hidden_grad, *new)


def solution(mesh):
    whole = P("rep", "dp", None)
    replicas, shards = mesh.shape["rep"], mesh.shape["dp"]

    def program(*args):
        return step(replicas, shards, *args)

    return jax.shard_map(
        program,
        mesh=mesh,
        in_specs=(P(None, "rep", "dp", None), P(), P(None, "dp"), P(None, "dp"), whole, whole, whole),
        out_specs=(P(None, "rep", "dp", None), whole, whole, whole),
        check_vma=False,
    )
```
